128 devices in a mesh: pix: 32 (over y, z, core), freq: 4 (over x).
Axes of the slice: x: 4, y: 4, z: 4, core: 2. Of those that a mesh axis runs over, the one named last changes fastest.
Arguments:
- cube: float32 [1024, 65536], P('freq', 'pix'), may hold values from -6 to 6
- probes: float32 [32, 65536], P(None, 'pix'), may hold values from -6 to 6
- galaxy: float32 [65536], P('pix'), may hold values from -6 to 6
- slices: int32 [65536], P('pix'), may hold values from 0 to 127
- valid: int32 [65536], P('pix'), may hold values 0 or 1
Outputs:
- cleaned: float32 [1024, 65536], P('freq', 'pix')
- cross: float32 [1024, 128], P('freq')
The draws below stay inside these ranges and needn't reach their ends.
All inputs are finite; a program needn't handle non-finite values. No bound on the sum of `valid` on one device may be relied on, other than what follows from the above.
Results may differ from the reference program's by a relative error of at most 0.00019.
Values sent between devices are 32-bit elements; how exact they have to be, the bound alone decides.
No kernel may reach another device: no remote copies, remote signals or barrier semaphores. Data moves between devices by JAX's collectives and lax.ppermute only.
A program may use at most 64 MiB of HBM per device.

```python
import jax
import jax.numpy as jnp
from jax import lax

F = 1024
K = 32
NS = 128
ITERS = 4
PIXELS = 65536


def touch_ends(drawn, stream_key, low, largest):
    longest = drawn.shape.index(max(drawn.shape))
    spots = []
    for shift in (0, 1):
        where = [jax.random.randint(jax.random.fold_in(stream_key, axis), (), 0, length) for axis, length in enumerate(drawn.shape)]
        where[longest] = (where[longest] + shift) % drawn.shape[longest]
        spots.append(tuple(where))
    return drawn.at[spots[0]].set(low).at[spots[1]].set(largest)


def level_of(key, dims, pieces, low, high):
    loudness = 1.0
    for position, shards_of in pieces:
        draws = jax.random.uniform(jax.random.fold_in(jax.random.fold_in(key, 6), position), (shards_of,), jnp.float32, low / len(pieces), high / len(pieces))
        loudness = loudness * jnp.repeat(jnp.exp(draws), dims[position] // shards_of).reshape((-1,) + (1,) * (len(dims) - 1 - position))
    return loudness


def scatter_about(rng, extent, deviation, bound, cuts=(), kind=jnp.bfloat16):
    entries = jax.random.normal(rng, extent, jnp.float32) * deviation
    if len(cuts) > 0:
        entries = level_of(rng, extent, cuts, -0.22, 0.18) * entries
    return jnp.clip(entries, min=-bound, max=bound).astype(kind)


def setup_inputs(seed: int = 0) -> dict:
    key_of = jax.random.split(jax.random.key(seed), 6)
    return {
        "cube": scatter_about(key_of[0], (F, PIXELS), 1.0, 6.0, ((0, 4), (1, 32)), jnp.float32),
        "probes": scatter_about(key_of[1], (K, PIXELS), 1.0, 6.0, ((1, 32),), jnp.float32),
        "galaxy": scatter_about(key_of[2], (PIXELS,), 1.0, 6.0, ((0, 32),), jnp.float32),
        "slices": touch_ends(jax.random.randint(key_of[3], (PIXELS,), 0, NS), jax.random.fold_in(key_of[3], 1), 0, NS - 1).astype(jnp.int32),
        "valid": touch_ends((jax.random.randint(key_of[4], (PIXELS,), 0, 4) < 3).astype(jnp.int32), jax.random.fold_in(key_of[4], 1), 0, 1),
    }


def multiply(left, right):
    return jnp.dot(left.astype(jnp.float32), right.astype(jnp.float32), precision=lax.Precision.HIGHEST, preferred_element_type=jnp.float32)

def orthonormal(factor):
    gram = multiply(factor.T, factor)
    lower = jnp.linalg.cholesky(gram)
    return lax.linalg.triangular_solve(lower, factor, left_side=False, lower=True, transpose_a=True)

def reference(cube, probes, galaxy, slices, valid):
    basis = orthonormal(multiply(cube, probes.T))
    for step in range(ITERS):
        amps = multiply(basis.T, cube)
        basis = orthonormal(multiply(cube, amps.T))
    amps = multiply(basis.T, cube)
    cleaned = cube - multiply(basis, amps)
    weights = galaxy * valid.astype(jnp.float32)
    table = (slices[:, None] == jnp.arange(NS, dtype=jnp.int32)[None, :]).astype(jnp.float32) * weights[:, None]
    cross = multiply(cleaned, table) * (float(PIXELS) / float(NS)) ** (-0.5)
    return (cleaned, cross)
```

```python
import functools

import jax
import jax.numpy as jnp
from jax import lax
from jax.experimental import pallas as pl
from jax.experimental.pallas import tpu as pltpu
from jax.sharding import Mesh, PartitionSpec as P

NS = 128
ITERS = 4
K = 32
T = 128
CHIPS = ("y", "z", "x")
HIGHEST = lax.Precision.HIGHEST
NN = (((1,), (0,)), ((), ()))
NT = (((1,), (1,)), ((), ()))
TN = (((0,), (0,)), ((), ()))


def multiply(left, right, dims=NN):
    return lax.dot_general(left, right, dims, precision=HIGHEST, preferred_element_type=jnp.float32)


def blocks_of(channels):
    count = channels // T
    return [(i, j) for i in range(count) for j in range(i, count)]


def rows_of(channels):
    gram = len(blocks_of(channels)) * T
    sketch = gram + K * channels // T
    return gram, sketch, sketch + channels


def gram_kernel(local_ref, probes_ref, weights_ref, slices_ref, out_ref):
    channels, width = local_ref.shape
    gram, sketch, total = rows_of(channels)
    position = {pair: index for index, pair in enumerate(blocks_of(channels))}
    step = 2 * T
    for top in range(0, channels, step):
        product = multiply(local_ref[top : top + step, :], local_ref[top:, :], NT)
        for half in range(2):
            i = top // T + half
            for j in range(i, channels // T):
                at = position[(i, j)] * T
                left = (j - top // T) * T
                out_ref[at : at + T, :] = product[half * T : half * T + T, left : left + T]
    sums = multiply(probes_ref[...], local_ref[...], NT)
    for j in range(channels // T):
        out_ref[gram + j * K : gram + (j + 1) * K, :] = sums[:, j * T : (j + 1) * T]
    levels = lax.broadcasted_iota(jnp.int32, (NS, width), 0)
    table = jnp.where(levels == slices_ref[...], weights_ref[...], 0.0)
    out_ref[sketch:total, :] = multiply(local_ref[...], table, NT)
    if total < out_ref.shape[0]:
        out_ref[total:, :] = jnp.zeros((out_ref.shape[0] - total, T), jnp.float32)


def orthonormal(factor):
    gram = multiply(factor, factor, NT)
    rows = lax.broadcasted_iota(jnp.int32, (K, T), 0)
    lanes = lax.broadcasted_iota(jnp.int32, (K, T), 1)
    unit = jnp.where(lanes == rows + K, 1.0, 0.0).astype(jnp.float32)
    wide = jnp.concatenate([gram, jnp.zeros((K, T - K), jnp.float32)], axis=1) + unit
    for k in range(K - 1):
        row = wide[k : k + 1, :]
        scaled = row / wide[k : k + 1, k : k + 1]
        column = jnp.where(rows[:, :1] > k, wide[:, k : k + 1], 0.0)
        wide = wide - column * scaled
    pivots = jnp.sum(jnp.where(lanes == rows, wide, 0.0), axis=1, keepdims=True)
    inverse = wide[:, K : 2 * K] * lax.rsqrt(pivots)
    return multiply(inverse, factor)


def iterate_kernel(scale, packed_ref, basis_ref, cross_ref, full):
    channels = basis_ref.shape[1]
    gram, sketch, total = rows_of(channels)
    for index, (i, j) in enumerate(blocks_of(channels)):
        block = packed_ref[index * T : (index + 1) * T, :]
        full[i * T : (i + 1) * T, j * T : (j + 1) * T] = block
        if i != j:
            full[j * T : (j + 1) * T, i * T : (i + 1) * T] = block.T
    factor = jnp.concatenate([packed_ref[gram + j * K : gram + (j + 1) * K, :] for j in range(channels // T)], axis=1)
    basis = orthonormal(factor)
    for step in range(ITERS):
        basis = orthonormal(multiply(basis, full[...]))
    basis_ref[...] = basis
    sums = packed_ref[sketch:total, :]
    inner = multiply(basis, sums)
    cross_ref[...] = (sums - multiply(basis, inner, TN)) * scale


def body(cube, probes, galaxy, slices, valid):
    nx, nc = lax.axis_size("x"), lax.axis_size("c")
    pixels = lax.axis_size("y") * lax.axis_size("z") * nc * cube.shape[1]
    scale = (float(pixels) / float(NS)) ** (-0.5)
    own, core = lax.axis_index("x"), lax.axis_index("c")
    rows, chips = cube.shape[0], lax.axis_size(CHIPS)
    channels = rows * nx
    local = lax.all_to_all(cube, "x", split_axis=1, concat_axis=0, tiled=True)
    width = local.shape[1]
    start = own * width
    weights = (galaxy * valid.astype(jnp.float32))[None, :]
    probe_cols = lax.dynamic_slice_in_dim(probes, start, width, 1)
    own_weights = lax.dynamic_slice_in_dim(weights, start, width, 1)
    own_slices = lax.dynamic_slice_in_dim(slices[None, :], start, width, 1)

    total = rows_of(channels)[2]
    piece = -(-total // (nc * chips * 8)) * 8
    packed = pl.pallas_call(
        gram_kernel,
        out_shape=jax.ShapeDtypeStruct((nc * chips * piece, T), jnp.float32),
        name="gram",
    )(local, probe_cols, own_weights, own_slices)

    swap = [(0, 1), (1, 0)]
    halves = packed.reshape(nc, chips * piece, T)
    mine = lax.dynamic_index_in_dim(halves, core, 0, keepdims=False)
    other = lax.dynamic_index_in_dim(halves, 1 - core, 0, keepdims=False)
    mine = mine + lax.ppermute(other, "c", swap)
    parts = lax.all_to_all(mine.reshape(chips, piece, T), CHIPS, 0, 0, tiled=True)
    owned = jnp.sum(parts, axis=0, keepdims=True)
    spread = jnp.broadcast_to(owned, (chips, piece, T))
    whole = lax.all_to_all(spread, CHIPS, 0, 0, tiled=True).reshape(chips * piece, T)
    partner = lax.ppermute(whole, "c", swap)
    low = jnp.where(core == 0, whole, partner)
    high = jnp.where(core == 0, partner, whole)
    packed = jnp.concatenate([low, high], axis=0)

    basis, cross = pl.pallas_call(
        functools.partial(iterate_kernel, scale),
        out_shape=(
            jax.ShapeDtypeStruct((K, channels), jnp.float32),
            jax.ShapeDtypeStruct((channels, NS), jnp.float32),
        ),
        scratch_shapes=[pltpu.VMEM((channels, channels), jnp.float32)],
        name="iterate",
    )(packed)
    amps = multiply(basis, local)
    amps = lax.all_to_all(jnp.broadcast_to(amps[None], (nx, K, width)), "x", 0, 0, tiled=True)
    amps = jnp.concatenate([amps[i] for i in range(nx)], axis=1)
    own_basis = lax.dynamic_slice_in_dim(basis, own * rows, rows, 1)
    cleaned = cube - multiply(own_basis, amps, TN)
    return (cleaned, lax.dynamic_slice_in_dim(cross, own * rows, rows, 0))


def solution(mesh):
    devices = mesh.devices.reshape(4, 4, 2, 4)
    pix = ("y", "z", "c")
    in_specs = (P("x", pix), P(None, pix), P(pix), P(pix), P(pix))
    out_specs = (P("x", pix), P("x", None))
    return jax.shard_map(body, mesh=Mesh(devices, ("y", "z", "c", "x")), in_specs=in_specs, out_specs=out_specs, check_vma=False)
```

```python
import functools

import jax
import jax.numpy as jnp
from jax import lax
from jax.experimental import pallas as pl
from jax.experimental.pallas import tpu as pltpu
from jax.sharding import Mesh, PartitionSpec as P

NS = 128
ITERS = 4
K = 32
T = 128
NX = 4
CHIPS = ("y", "z", "x")
SWAP = [(0, 1), (1, 0)]
NN = (((1,), (0,)), ((), ()))
NT = (((1,), (1,)), ((), ()))
TN = (((0,), (0,)), ((), ()))
F32 = jnp.float32

NEXT = 0
SKIP = NEXT + NX * 2 * T
DIAG = SKIP + 2 * 2 * T
SIDE = DIAG + NX * T
SKETCH = SIDE + 2 * T
TABLE = SKETCH + NX * K
USED = TABLE + NX * T

VMEM = pl.BlockSpec(memory_space=pltpu.VMEM)
SMEM = pl.BlockSpec(memory_space=pltpu.SMEM)


def dot(left, right, dims=NN):
    return lax.dot_general(left, right, dims, preferred_element_type=F32)


def split(value):
    high = value.astype(jnp.bfloat16)
    rest = value - high.astype(F32)
    mid = rest.astype(jnp.bfloat16)
    return high, mid, (rest - mid.astype(F32)).astype(jnp.bfloat16)


def product(left, right, dims):
    rows = left[0].shape[0]
    one = dot(left[0], right[2], dims)
    two = dot(jnp.concatenate(left[:2], axis=0), right[1], dims)
    three = dot(jnp.concatenate(left, axis=0), right[0], dims)
    small = one + two[rows:] + three[2 * rows :]
    return small + (two[:rows] + three[rows : 2 * rows]) + three[:rows]


def gram_kernel(rels, new, pairs, first, meta_ref, aux_ref, aux_partner_ref, *refs):
    count = len(rels)
    pieces, rest = refs[: 2 * count], refs[2 * count :]
    if not first:
        rest[1][...] = rest[0][...]
        rest = rest[1:]
    out_ref, terms = rest
    own, core = meta_ref[0], meta_ref[1]
    for index in range(count):
        for side in range(2):
            for term, value in enumerate(split(pieces[2 * index + side][...])):
                width = value.shape[1]
                terms[index, term, :, side * width : (side + 1) * width] = value

    def whole(index):
        return tuple(terms[index, term] for term in range(3))

    def half(index):
        return tuple(terms[index, term, pl.ds(pl.multiple_of(core * T, T), T), :] for term in range(3))

    def store(base, at, value):
        size = value.shape[0]
        out_ref[pl.ds(pl.multiple_of(base + at * size, size), size), :] = value

    aux = jnp.concatenate([aux_ref[...], aux_partner_ref[...]], axis=1)
    probes = split(aux[:K])
    levels = lax.broadcasted_iota(jnp.int32, (NS, aux.shape[1]), 0).astype(F32)
    table = split(jnp.where(levels == aux[K + 1 : K + 2], aux[K : K + 1], 0.0))
    for rel in new:
        index = rels.index(rel)
        block = lax.rem(own - rel + NX, NX)
        mine = half(index)
        square = product(mine, whole(index), NT)
        left, right = square[:, :T], square[:, T:]
        store(DIAG, block, jnp.where(core == 0, left, right))

        @pl.when((block < 2) == (core == 0))
        def _():
            store(SIDE, lax.rem(block, 2), jnp.where(core == 0, right, left))

        store(TABLE, block, product(mine, table, NT))
        store(SKETCH, block, product(probes, mine, NT))
    for rows, columns, near in pairs:
        low, high = rels.index(rows), rels.index(columns)
        block = lax.rem(own - rows + NX, NX)
        if near:
            result = product(half(low), whole(high), NT)
            base = NEXT
        else:
            flip = block >= 2
            block = lax.rem(block, 2)
            low, high = jnp.where(flip, high, low), jnp.where(flip, low, high)
            result = product(half(low), whole(high), NT)
            base = SKIP
        size = result.shape[0]
        at = pl.multiple_of(base + block * 2 * size, 2 * size)
        out_ref[pl.ds(at, size), :] = result[:, :T]
        out_ref[pl.ds(at + size, size), :] = result[:, T:]
    if first and USED < out_ref.shape[0]:
        out_ref[USED:, :] = jnp.zeros((out_ref.shape[0] - USED, T), F32)


def inverse_factor(gram, panel=16):
    rows = lax.broadcasted_iota(jnp.int32, (K, T), 0)
    lanes = lax.broadcasted_iota(jnp.int32, (K, T), 1)
    unit = jnp.where(lanes == rows + K, 1.0, 0.0).astype(F32)
    wide = jnp.concatenate([gram, jnp.zeros((K, T - K), F32)], axis=1) + unit
    for base in range(0, K, panel):
        columns = [jnp.broadcast_to(wide[:, base + j : base + j + 1], (K, T)) for j in range(panel)]
        for j in range(panel):
            k = base + j
            if k == K - 1:
                break
            inverse = 1.0 / columns[j][k : k + 1, :]
            below = jnp.where(rows > k, columns[j], 0.0)
            scaled = wide[k : k + 1, :] * inverse
            heads = [columns[i][k : k + 1, :] * inverse for i in range(j + 1, panel)]
            wide = wide - below * scaled
            for head, i in zip(heads, range(j + 1, panel)):
                columns[i] = columns[i] - below * head
    pivots = jnp.sum(jnp.where(lanes == rows, wide, 0.0), axis=1, keepdims=True)
    return wide[:, K : 2 * K] * lax.rsqrt(pivots)


def gram_of(terms):
    stacked = jnp.concatenate(terms, axis=0)
    all_pairs = dot(stacked, stacked, NT)

    def part(i, j):
        return all_pairs[i * K : (i + 1) * K, j * K : (j + 1) * K]

    return (part(0, 2) + part(2, 0) + part(1, 1)) + (part(0, 1) + part(1, 0)) + part(0, 0)


def deep(terms, order, axis):
    return jnp.concatenate([terms[i] for i in order], axis=axis)


LEFT = (2, 1, 0, 1, 0, 0)
RIGHT = (0, 1, 2, 0, 1, 0)


def iterate_kernel(scale, meta_ref, mine_ref, partner_ref, r0, r1, r2, r3, amps_ref, own_basis_ref, cross_ref, full, basis_ref, sums_ref):
    own, core = meta_ref[0], meta_ref[1]
    locals_ = (r0, r1, r2, r3)

    def load(side, at, size):
        same = mine_ref[at : at + size, :]
        other = partner_ref[at : at + size, :]
        return jnp.where(core == side, same, other)

    def place(row, column, value):
        for term, part in enumerate(split(value)):
            full[term, row : row + value.shape[0], column : column + value.shape[1]] = part

    step = 2 * T
    factor = jnp.concatenate([load(side, SKETCH + a * K, K) for a in range(NX) for side in range(2)], axis=1)
    for side in range(2):
        for a in range(NX):
            row = a * step + side * T
            place(row, row, load(side, DIAG + a * T, T))
            sums_ref[row : row + T, :] = load(side, TABLE + a * T, T)
            if (a < 2) == (side == 0):
                value = load(side, SIDE + (a % 2) * T, T)
                column = a * step + (1 - side) * T
                place(row, column, value)
                place(column, row, value.T)
            spans = [(NEXT + a * step, (a + 1) % NX)]
            if a < 2:
                spans.append((SKIP + a * step, a + 2))
            for at, b in spans:
                for part in range(2):
                    value = load(side, at + part * T, T)
                    column = b * step + part * T
                    place(row, column, value)
                    place(column, row, value.T)
    for iteration in range(ITERS + 1):
        terms = split(factor)
        inverse = inverse_factor(gram_of(terms))
        ahead = factor
        if iteration < ITERS:
            ahead = product(terms, (full[0], full[1], full[2]), NN)
        factor = dot(deep(split(inverse), LEFT, 1), deep(split(ahead), RIGHT, 0))
    basis_ref[...] = factor
    amps = jnp.zeros(amps_ref.shape, F32)
    for rel in range(NX):
        block = lax.rem(own - rel + NX, NX)
        rows = basis_ref[:, pl.ds(pl.multiple_of(block * step, step), step)]
        amps = amps + product(split(rows), split(locals_[rel][...]), NN)
    amps_ref[...] = amps
    at = pl.multiple_of(own * step, step)
    own_basis = basis_ref[:, pl.ds(at, step)]
    own_basis_ref[...] = own_basis
    inner = product(split(factor), split(sums_ref[...]), NN)
    fitted = dot(deep(split(own_basis), LEFT, 0), deep(split(inner), RIGHT, 0), TN)
    cross_ref[...] = (sums_ref[pl.ds(at, step), :] - fitted) * scale


def clean_kernel(meta_ref, basis_ref, a0, a1, a2, a3, cube_ref, out_ref):
    rel = lax.rem(meta_ref[0] - pl.program_id(0) + NX, NX)
    amps = jnp.where(rel < 2, jnp.where(rel == 0, a0[...], a1[...]), jnp.where(rel == 2, a2[...], a3[...]))
    fitted = dot(deep(split(basis_ref[...]), LEFT, 0), deep(split(amps), RIGHT, 0), TN)
    out_ref[...] = cube_ref[...] - fitted


def body(cube, probes, galaxy, slices, valid):
    chips = lax.axis_size(CHIPS)
    rows, columns = cube.shape
    pixels = chips // NX * 2 * columns
    scale = (float(pixels) / float(NS)) ** (-0.5)
    own, core = lax.axis_index("x"), lax.axis_index("c")
    meta = jnp.stack([own, core]).astype(jnp.int32)
    width = columns // NX

    def shift(value, by):
        return lax.ppermute(value, "x", [(i, (i + by) % NX) for i in range(NX)])

    def columns_of(value, block):
        return lax.dynamic_slice_in_dim(value, block * width, width, 1)

    received = [columns_of(cube, own)]
    for by in range(1, NX):
        received.append(shift(columns_of(cube, lax.rem(own + by, NX)), by))
    partner = [lax.ppermute(piece, "c", SWAP) for piece in received]
    weights = galaxy * valid.astype(F32)
    extra = jnp.zeros((8, columns), F32).at[0].set(weights).at[1].set(slices.astype(F32))
    aux = columns_of(jnp.concatenate([probes, extra], axis=0), own)
    aux_partner = lax.ppermute(aux, "c", SWAP)

    piece = -(-USED // (chips * 8)) * 8
    shape = jax.ShapeDtypeStruct((chips * piece, T), F32)

    def gram(rels, new, pairs, packed):
        first = packed is None
        blocks = [value for rel in rels for value in (received[rel], partner[rel])]
        args = [meta, aux, aux_partner] + blocks + ([] if first else [packed])
        return pl.pallas_call(
            functools.partial(gram_kernel, rels, new, pairs, first),
            out_shape=shape,
            in_specs=[SMEM] + [VMEM] * (len(args) - 1),
            out_specs=VMEM,
            scratch_shapes=[pltpu.VMEM((len(rels), 3, rows, 2 * width), jnp.bfloat16)],
            name="gram",
        )(*args)

    packed = gram((0, 1), (0, 1), ((1, 0, True),), None)
    packed = gram((0, 1, 3), (3,), ((0, 3, True), (1, 3, False)), packed)
    packed = gram((0, 1, 3, 2), (2,), ((2, 1, True), (3, 2, True), (0, 2, False)), packed)

    parts = lax.all_to_all(packed.reshape(chips, piece, T), CHIPS, 0, 0, tiled=True)
    owned = jnp.sum(parts, axis=0, keepdims=True)
    spread = jnp.broadcast_to(owned, (chips, piece, T))
    mine = lax.all_to_all(spread, CHIPS, 0, 0, tiled=True).reshape(chips * piece, T)
    other = lax.ppermute(mine, "c", SWAP)

    channels = rows * NX
    amps, own_basis, cross = pl.pallas_call(
        functools.partial(iterate_kernel, scale),
        out_shape=(
            jax.ShapeDtypeStruct((K, width), F32),
            jax.ShapeDtypeStruct((K, rows), F32),
            jax.ShapeDtypeStruct((rows, NS), F32),
        ),
        in_specs=[SMEM] + [VMEM] * 6,
        out_specs=(VMEM, VMEM, VMEM),
        scratch_shapes=[
            pltpu.VMEM((3, channels, channels), jnp.bfloat16),
            pltpu.VMEM((K, channels), F32),
            pltpu.VMEM((channels, NS), F32),
        ],
        name="iterate",
    )(meta, mine, other, *received)
    spread_amps = [amps] + [shift(amps, by) for by in range(1, NX)]
    block = pl.BlockSpec((rows, width), lambda j: (0, j))
    cleaned = pl.pallas_call(
        clean_kernel,
        grid=(NX,),
        out_shape=jax.ShapeDtypeStruct(cube.shape, F32),
        in_specs=[SMEM] + [VMEM] * 5 + [block],
        out_specs=block,
        name="clean",
    )(meta, own_basis, *spread_amps, cube)
    return (cleaned, cross)


def solution(mesh):
    devices = mesh.devices.reshape(4, 4, 2, NX)
    pix = ("y", "z", "c")
    in_specs = (P("x", pix), P(None, pix), P(pix), P(pix), P(pix))
    out_specs = (P("x", pix), P("x", None))
    return jax.shard_map(body, mesh=Mesh(devices, ("y", "z", "c", "x")), in_specs=in_specs, out_specs=out_specs, check_vma=False)
```
